32 devices in a mesh: req: 16 (over z, x, core), tp: 2 (over y).
Axes of the slice: x: 2, y: 2, z: 4, core: 2. Of those that a mesh axis runs over, the one named last changes fastest.
Arguments:
- state: bfloat16 [256, 2048], P('req'), may hold values from -3 to 3
- norm_gain: float32 [2048], replicated, may hold values from 0.25 to 4
- w_qkv: bfloat16 [2048, 2, 512], P(None, 'tp'), may hold values from -0.125 to 0.125
- w_out: bfloat16 [2, 256, 2048], P('tp'), may hold values from -0.25 to 0.25
- kv_cache: bfloat16 [2944, 2, 16, 256], P('req', 'tp')
- lengths: int32 [256], P('req'), may hold values from 32 to 1024, as said below
- page_table: int32 [256, 64], P('req'), may hold values from 0 to 183, as said below
- dest_slot: int32 [256], P('req'), may hold values from 0 to 255, as said below
Outputs:
- new_state: bfloat16 [256, 2048], P('req')
The draws below stay inside these ranges and needn't reach their ends.
Inputs may be any that keep to these rules, and one draw needn't show every extreme that they name: `lengths`: each device of req holds at most one request with more than 128 cached tokens; all others have 32 to 128; in every draw some request has exactly 1024. `page_table`: entry j of row r, for j below ceil(lengths[r] / 16), is the page (numbered within the home device r // 16) holding tokens j * 16 to (j + 1) * 16 - 1 of request r; no page serves two such entries; the entries after those are 183. dest_slot is a permutation. The request in slot k of device i of req (index i * 16 + k) goes to slot k of device (i + o_k) mod (16), with offsets o_k the same for all devices; at most 2 requests of one device go to one device, and exactly 2 do for some pairs.
All inputs are finite; a program needn't handle non-finite values.
Results may differ from the reference program's by a relative error of at most 0.01.
Values may be sent and summed in bfloat16 or wider, within the bound.
A program may use at most 64 MiB of HBM per device.

```python
import math
import jax
import jax.numpy as jnp
from jax import lax

D = 2048
HD = 128
GROUP = 2
REQ_DEV = 16
PAGE = 16
SHORT_LO = 32
SHORT_HI = 128
LONG_MAX = 1024
KVH = 2
MAXP = 64
PAGES_DEV = 184
PAGES = 2944
REQS = 256


def request_layout(key):
    base_key = jax.random.fold_in(key, 11)
    keys = jax.random.split(base_key, 6)
    device_count = REQS // REQ_DEV
    short_len = jax.random.randint(keys[0], (device_count, REQ_DEV), SHORT_LO, SHORT_HI + 1)
    has_long = jax.random.randint(keys[1], (device_count,), 0, 2)
    forced = jax.random.randint(keys[2], (), 0, device_count)
    device_ids = jnp.arange(device_count)
    has_long = jnp.where(device_ids == forced, 1, has_long)
    long_len = LONG_MAX - jax.random.randint(keys[3], (device_count,), 0, LONG_MAX // 2)
    long_len = jnp.where(device_ids == forced, LONG_MAX, long_len)
    long_slot = jax.random.randint(keys[4], (device_count,), 0, REQ_DEV)
    is_long = (has_long[:, None] == 1) & (jnp.arange(REQ_DEV)[None, :] == long_slot[:, None])
    req_len = jnp.where(is_long, long_len[:, None], short_len).astype(jnp.int32)
    page_count = (req_len + PAGE - 1) // PAGE
    perm_keys = jax.random.split(keys[5], device_count)
    orders = jax.vmap(lambda one_key: jax.random.permutation(one_key, PAGES_DEV))(perm_keys)
    starts = jnp.cumsum(page_count, axis=1) - page_count
    index_grid = starts[:, :, None] + jnp.arange(MAXP)[None, None, :]
    valid = jnp.arange(MAXP)[None, None, :] < page_count[:, :, None]
    clipped = jnp.clip(index_grid, 0, PAGES_DEV - 1).reshape(device_count, REQ_DEV * MAXP)
    table = jnp.take_along_axis(orders, clipped, axis=1).reshape(device_count, REQ_DEV, MAXP)
    table = jnp.where(valid, table, PAGES_DEV - 1).astype(jnp.int32)
    return (req_len.reshape(REQS), table.reshape(REQS, MAXP))


def draw_lengths(key, part):
    return request_layout(key)[0]


def draw_page_table(key, part):
    return request_layout(key)[1]


def draw_dest_slot(key, part):
    device_count = REQS // REQ_DEV
    half_way = device_count // 2
    order = jax.random.permutation(jax.random.fold_in(key, 23), device_count - 1)
    order = jnp.where(order >= half_way, order + 1, order)
    paired = jnp.full((2,), half_way, dtype=order.dtype)
    offsets = jnp.concatenate([paired, order[:REQ_DEV - 2]])
    devices = jnp.arange(device_count)[:, None]
    target = (devices + offsets[None, :]) % device_count * REQ_DEV + jnp.arange(REQ_DEV)[None, :]
    return target.reshape(REQS).astype(jnp.int32)


def draw_kv_cache(key, part):
    keys = jax.random.split(jax.random.fold_in(key, 5), 1)
    shape = (PAGES, KVH, PAGE, 2 * HD)
    base = jax.random.normal(keys[0], shape, jnp.float32)
    return base.astype(jnp.bfloat16)


def block_scale(stream_key, extent, cuts, low, largest):
    level = 1.0
    for position, blocks in cuts:
        steps = jax.random.uniform(jax.random.fold_in(jax.random.fold_in(stream_key, 6), position), (blocks,), jnp.float32, low / len(cuts), largest / len(cuts))
        level = level * jnp.repeat(jnp.exp(steps), extent[position] // blocks).reshape((-1,) + (1,) * (len(extent) - 1 - position))
    return level


def gaussian(stream_key, shape, width, bound, cuts=(), kind=jnp.bfloat16):
    level = block_scale(stream_key, shape, cuts, -0.22, 0.18) if cuts else 1.0
    entries = jax.random.normal(stream_key, shape, jnp.float32) * width * level
    return jnp.minimum(jnp.maximum(entries, -bound), bound).astype(kind)


def setup_inputs(seed: int = 0) -> dict:
    splits = jax.random.split(jax.random.key(seed), 9)
    return {
        "state": gaussian(splits[0], (REQS, D), 0.5, 3.0, ((0, 16),)),
        "norm_gain": jnp.clip(jnp.exp(jax.random.uniform(splits[1], (D,), jnp.float32, math.log(0.25), math.log(4.0))), 0.25, 4.0),
        "w_qkv": gaussian(splits[2], (D, KVH, (GROUP + 2) * HD), D ** -0.5, 0.125, ((1, 2),)),
        "w_out": gaussian(splits[3], (KVH, GROUP * HD, D), (KVH * GROUP * HD) ** -0.5, 0.25, ((0, 2),)),
        "kv_cache": draw_kv_cache(jax.random.fold_in(splits[8], 71), 0),
        "lengths": draw_lengths(jax.random.fold_in(splits[8], 71), 0),
        "page_table": draw_page_table(jax.random.fold_in(splits[8], 71), 0),
        "dest_slot": draw_dest_slot(jax.random.fold_in(splits[8], 71), 0),
    }


def normalize(values, scale_gain):
    wide = values.astype(jnp.float32)
    factor = lax.rsqrt(lax.optimization_barrier(jnp.mean(wide * wide, axis=-1, keepdims=True)) + 1e-05)
    return (wide * factor * scale_gain).astype(jnp.bfloat16)

def rotate(values, positions):
    half_size = values.shape[-1] // 2
    freqs = jnp.exp(-jnp.log(1000000.0) * 2.0 * jnp.arange(half_size, dtype=jnp.float32) / (2 * half_size))
    angles = positions.astype(jnp.float32)[:, None, None] * freqs
    cosine = jnp.cos(angles)
    sine = jnp.sin(angles)
    first = values[..., :half_size]
    second = values[..., half_size:]
    return jnp.concatenate([first * cosine - second * sine, second * cosine + first * sine], axis=-1)

def reference(state, norm_gain, w_qkv, w_out, kv_cache, lengths, page_table, dest_slot):
    total_rows = state.shape[0]
    devices_req = total_rows // REQ_DEV
    normed = normalize(state, norm_gain)
    proj = jnp.einsum('rd,dgc->rgc', normed.astype(jnp.float32), w_qkv.astype(jnp.float32))
    query = rotate(proj[..., :GROUP * HD].reshape(total_rows, KVH * GROUP, HD), lengths)
    query = query.astype(jnp.bfloat16).reshape(total_rows, KVH, GROUP, HD)
    new_key = rotate(proj[..., GROUP * HD:(GROUP + 1) * HD], lengths).astype(jnp.bfloat16)
    new_value = proj[..., (GROUP + 1) * HD:].astype(jnp.bfloat16)
    scale = 1.0 / jnp.sqrt(jnp.float32(HD))

    def per_device(inputs):
        dev_query, dev_key, dev_value, dev_len, dev_table, dev_pool = inputs
        picked = dev_pool[dev_table]
        picked = jnp.transpose(picked, (0, 2, 1, 3, 4)).reshape(REQ_DEV, KVH, MAXP * PAGE, 2 * HD)
        scores = jnp.einsum('rgjc,rgtc->rgjt', dev_query.astype(jnp.float32), picked[..., :HD].astype(jnp.float32)) * scale
        live = jnp.arange(MAXP * PAGE, dtype=jnp.int32)[None, :] < dev_len[:, None]
        scores = jnp.where(live[:, None, None, :], scores, -jnp.inf)
        score_new = jnp.einsum('rgjc,rgc->rgj', dev_query.astype(jnp.float32), dev_key.astype(jnp.float32)) * scale
        row_top = jnp.maximum(lax.optimization_barrier(jnp.max(scores, axis=-1)), score_new)
        weights = jnp.exp(scores - row_top[..., None])
        weight_new = jnp.exp(score_new - row_top)
        total = lax.optimization_barrier(jnp.sum(weights, axis=-1)) + weight_new
        numer = jnp.einsum('rgjt,rgtc->rgjc', weights.astype(jnp.bfloat16).astype(jnp.float32), picked[..., HD:].astype(jnp.float32))
        numer = numer + weight_new.astype(jnp.bfloat16).astype(jnp.float32)[..., None] * dev_value.astype(jnp.float32)[:, :, None, :]
        return (numer / total[..., None]).astype(jnp.bfloat16).reshape(REQ_DEV, KVH, GROUP * HD)
    attn = lax.map(per_device, (query.reshape(devices_req, REQ_DEV, KVH, GROUP, HD), new_key.reshape(devices_req, REQ_DEV, KVH, HD), new_value.reshape(devices_req, REQ_DEV, KVH, HD), lengths.reshape(devices_req, REQ_DEV), page_table.reshape(devices_req, REQ_DEV, MAXP), kv_cache.reshape(devices_req, PAGES_DEV, KVH, PAGE, 2 * HD)))
    attn = attn.reshape(total_rows, KVH, GROUP * HD)
    output = jnp.einsum('rgc,gcd->rd', attn.astype(jnp.float32), w_out.astype(jnp.float32))
    mixed = (state.astype(jnp.float32) + output).astype(jnp.bfloat16)
    return jnp.zeros_like(mixed).at[dest_slot].set(mixed)
```

```python
import functools
import math

import jax
import jax.numpy as jnp
from jax import lax
from jax.experimental import pallas as pl
from jax.experimental.pallas import tpu as pltpu
from jax.sharding import PartitionSpec as P

MESH = pl.DeviceIdType.MESH
LANES = 128
F32 = jnp.float32
BF16 = jnp.bfloat16


def iota(shape, axis):
    return lax.broadcasted_iota(jnp.int32, shape, axis)


def to_column(row):
    size = row.shape[1]
    eye = iota((size, size), 0) == iota((size, size), 1)
    return jnp.sum(jnp.where(eye, jnp.broadcast_to(row, (size, size)), 0.0), axis=1, keepdims=True)


def kernel(
    n,
    tp,
    page,
    state_hbm,
    gain_hbm,
    wqkv_hbm,
    wout_hbm,
    pool_hbm,
    len_hbm,
    table_hbm,
    dest_hbm,
    out_ref,
    state_ref,
    gain_ref,
    len_ref,
    table_ref,
    dest_ref,
    wqkv,
    wout,
    pool,
    outgoing,
    incoming,
    heads_out,
    heads_in,
    load_sem,
    move_send,
    move_recv,
):
    rows, width = state_ref.shape
    group = wout.shape[0] // LANES
    chunk = width // tp
    blocks = chunk // LANES
    tokens = pool.shape[0]
    page_count = tokens // page
    me = lax.axis_index("req")
    my_part = lax.axis_index("tp")

    steps = 4
    depth = width // steps
    loads = []
    for step in range(steps):
        span = pl.ds(step * depth, depth)
        loads.append(pltpu.make_async_copy(wqkv_hbm.at[span], wqkv.at[span], load_sem.at[step]))
    load_pool = pltpu.make_async_copy(pool_hbm, pool, load_sem.at[steps])
    load_wout = pltpu.make_async_copy(wout_hbm, wout, load_sem.at[steps + 1])
    small = []
    for slot, (src, dst) in enumerate(
        (
            (state_hbm, state_ref),
            (gain_hbm, gain_ref),
            (len_hbm, len_ref),
            (table_hbm, table_ref),
            (dest_hbm, dest_ref),
        )
    ):
        small.append(pltpu.make_async_copy(src, dst, load_sem.at[steps + 2 + slot]))
    for load in small + loads:
        load.start()
    load_pool.start()
    load_wout.start()

    barrier = pltpu.get_barrier_semaphore()

    def wrapped(value, size):
        return jnp.where(value >= size, value - size, value)

    def each_request_device(act):
        if n <= 32:
            for peer in range(n):
                act(peer)
        else:
            pl.loop(0, n)(act)

    def each_other(act):
        def visit(peer):
            pl.when(me != peer)(lambda: act(peer))

        each_request_device(visit)

    def device(peer, shift):
        return {"req": peer, "tp": wrapped(my_part + shift, tp)}

    def greet(shift, peer):
        pl.semaphore_signal(barrier, inc=1, device_id=device(peer, shift), device_id_type=MESH)

    each_other(functools.partial(greet, 0))
    for shift in range(1, tp):
        each_request_device(functools.partial(greet, shift))


    for load in small:
        load.wait()

    wide = state_ref[...].astype(F32)
    factor = lax.rsqrt(jnp.mean(wide * wide, axis=-1, keepdims=True) + 1e-05)
    normed = (wide * factor * gain_ref[...]).astype(BF16)

    length = to_column(len_ref[...].astype(F32))
    lane = iota((rows, LANES), 1)
    half = LANES // 2
    index = lax.rem(lane, half).astype(F32)
    freqs = jnp.exp(-math.log(1000000.0) * 2.0 * index / LANES)
    angles = length * freqs
    cosine = jnp.cos(angles)
    sine = jnp.sin(angles)
    sine = jnp.where(lane < half, -sine, sine)

    used = jnp.floor((length + (page - 1)) / page).astype(jnp.int32)
    table = table_ref[...]
    table = jnp.where(iota(table.shape, 1) < used, table, -1)
    padded = pl.cdiv(page_count, LANES) * LANES
    page_id = iota((rows, padded), 1)
    live_count = jnp.zeros((rows, padded), F32)
    for entry in range(table.shape[1]):
        left = length - float(entry * page)
        live_count = jnp.where(page_id == table[:, entry : entry + 1], left, live_count)
    live_count = jnp.clip(live_count, 0.0, float(page))
    per_block = LANES // page
    shifted = []
    for block in range(tokens // LANES):
        first = block * per_block
        base = first // LANES * LANES
        piece = live_count[:, base : base + LANES]
        if first != base:
            piece = pltpu.roll(piece, LANES - (first - base), 1)
        shifted.append(piece)
    spread = (iota((LANES, LANES), 0) == iota((LANES, LANES), 1) // page).astype(BF16)
    live_tokens = jnp.dot(
        jnp.concatenate(shifted, axis=0).astype(BF16), spread, preferred_element_type=F32
    )

    shift_bits = rows.bit_length() - 1
    target_row = lax.shift_right_logical(dest_ref[...], shift_bits).astype(F32)
    target = to_column(target_row)
    same = jnp.broadcast_to(target, (rows, rows)) == jnp.broadcast_to(target_row, (rows, rows))
    earlier = iota((rows, rows), 1) < iota((rows, rows), 0)
    rank = jnp.sum(jnp.where(same & earlier, 1.0, 0.0), axis=1, keepdims=True)
    source = (2 * me).astype(F32) - target
    source = jnp.where(source < 0, source + n, source)
    source = jnp.where(source >= n, source - n, source)
    key_out = (target * 2 + rank).astype(jnp.int32)
    key_in = (source * 2 + rank).astype(jnp.int32)
    def packing(parts, depth):
        flat = rows * parts
        picked = iota((rows, flat), 0) == lax.rem(iota((rows, flat), 1), rows)
        key_row = jnp.sum(
            jnp.where(picked, key_out, 0).astype(F32), axis=0, keepdims=True
        ).astype(jnp.int32)
        row_id = iota((n * depth, flat), 0)
        within = lax.rem(row_id, depth)
        slot_id = row_id // depth * 2 + within // parts
        pack = (
            (slot_id == key_row)
            & (within < 2 * parts)
            & (lax.rem(within, parts) == iota((n * depth, flat), 1) // rows)
        ).astype(BF16)
        key_col = jnp.concatenate([key_in] * parts, axis=0)
        col_id = iota((flat, n * depth), 1)
        within = lax.rem(col_id, depth)
        slot_id = col_id // depth * 2 + within // parts
        unpack = (
            (slot_id == key_col)
            & (within < 2 * parts)
            & (lax.rem(within, parts) == iota((flat, n * depth), 0) // rows)
        ).astype(BF16)
        return pack, unpack

    piece_rows = 2 * blocks
    head_rows = heads_out.shape[1]
    pack, unpack = packing(blocks, piece_rows)
    pack_heads, unpack_heads = packing(group, head_rows)

    proj = None
    for step in range(steps):
        loads[step].wait()
        span = slice(step * depth, (step + 1) * depth)
        term = jnp.dot(normed[:, span], wqkv[span, :], preferred_element_type=F32)
        proj = term if proj is None else proj + term

    def rotated(values):
        return (values * cosine + pltpu.roll(values, half, 1) * sine).astype(BF16)

    heads = [rotated(proj[:, g * LANES : (g + 1) * LANES]) for g in range(group)]
    new_key = rotated(proj[:, group * LANES : (group + 1) * LANES])
    new_value = proj[:, (group + 1) * LANES :].astype(BF16)
    query = jnp.concatenate(heads, axis=0)

    scale = 1.0 / math.sqrt(LANES)
    load_pool.wait()
    scores = lax.dot_general(
        query, pool[:, :LANES], (((1,), (1,)), ((), ())), preferred_element_type=F32
    )
    offset = lax.rem(lane, page).astype(F32)
    masked = []
    for block in range(tokens // LANES):
        live = live_tokens[block * rows : (block + 1) * rows] > offset
        piece = scores[:, block * LANES : (block + 1) * LANES] * scale
        masked.append(
            jnp.concatenate(
                [
                    jnp.where(live, piece[g * rows : (g + 1) * rows], -jnp.inf)
                    for g in range(group)
                ],
                axis=0,
            )
        )
    scores = jnp.concatenate(masked, axis=1)
    keys = jnp.concatenate([new_key] * group, axis=0).astype(F32)
    values = jnp.concatenate([new_value] * group, axis=0).astype(F32)
    score_new = jnp.sum(query.astype(F32) * keys, axis=1, keepdims=True) * scale
    top = jnp.maximum(jnp.max(scores, axis=1, keepdims=True), score_new)
    weights = jnp.exp(scores - top)
    weight_new = jnp.exp(score_new - top)
    total = jnp.sum(weights, axis=1, keepdims=True) + weight_new
    numer = jnp.dot(weights.astype(BF16), pool[:, LANES:], preferred_element_type=F32)
    numer = numer + weight_new.astype(BF16).astype(F32) * values
    attn = (numer / total).astype(BF16)

    packed = jnp.dot(pack_heads, attn, preferred_element_type=F32)
    heads_out[...] = packed.reshape(n, head_rows, LANES).astype(BF16)
    pl.semaphore_wait(barrier, n * tp - 1)

    def send_heads(peer):
        pltpu.make_async_remote_copy(
            src_ref=heads_out.at[peer],
            dst_ref=heads_in.at[me],
            send_sem=move_send.at[0],
            recv_sem=move_recv.at[0],
            device_id=device(peer, 0),
            device_id_type=MESH,
        ).start()

    each_other(send_heads)

    load_wout.wait()
    attn = jnp.concatenate([attn[g * rows : (g + 1) * rows] for g in range(group)], axis=1)
    term = jnp.dot(attn, wout[...], preferred_element_type=F32)
    mixed = (state_ref[...].astype(F32) * (1.0 / (tp - 1)) + term).astype(BF16)
    for part in range(tp):
        first = part * chunk
        stacked = jnp.concatenate(
            [mixed[:, first + b * LANES : first + (b + 1) * LANES] for b in range(blocks)], axis=0
        )
        packed = jnp.dot(pack, stacked, preferred_element_type=F32)
        outgoing[:, part * piece_rows : (part + 1) * piece_rows] = packed.reshape(
            n, piece_rows, LANES
        ).astype(BF16)

    def send(shift, peer):
        pltpu.make_async_remote_copy(
            src_ref=outgoing.at[peer],
            dst_ref=incoming.at[(shift - 1) * n + me],
            send_sem=move_send.at[1],
            recv_sem=move_recv.at[1],
            device_id=device(peer, shift),
            device_id_type=MESH,
        ).start()

    for shift in range(1, tp):
        each_request_device(functools.partial(send, shift))

    heads_in[me] = heads_out[me]
    others = heads_in.at[pl.ds(0, n - 1)]
    pltpu.make_async_copy(others, others, move_recv.at[0]).wait()
    received = heads_in[...].astype(F32).reshape(n * head_rows, LANES).astype(BF16)
    arrived = jnp.dot(unpack_heads, received, preferred_element_type=F32).astype(BF16)
    arrived = jnp.concatenate([arrived[g * rows : (g + 1) * rows] for g in range(group)], axis=1)
    own = jnp.dot(arrived, wout[...], preferred_element_type=F32)

    pltpu.make_async_copy(incoming, incoming, move_recv.at[1]).wait()
    total_rows = n * piece_rows
    for part in range(tp):
        moved = None
        for origin in range(tp - 1):
            received = incoming[
                origin * n : (origin + 1) * n, part * piece_rows : (part + 1) * piece_rows
            ].astype(F32)
            received = received.reshape(total_rows, LANES).astype(BF16)
            taken = jnp.dot(unpack, received, preferred_element_type=F32)
            moved = taken if moved is None else moved + taken
        for b in range(blocks):
            first = part * chunk + b * LANES
            out_ref[:, first : first + LANES] = (
                moved[b * rows : (b + 1) * rows] + own[:, first : first + LANES]
            ).astype(BF16)
    pltpu.make_async_copy(others, others, move_send.at[0]).wait()
    pltpu.make_async_copy(incoming, incoming, move_send.at[1]).wait()


def local(n, tp, state, norm_gain, w_qkv, w_out, kv_cache, lengths, page_table, dest_slot):
    rows, width = state.shape
    page_count, _, page, entry = kv_cache.shape
    tokens = page_count * page
    chunk = width // tp
    blocks = chunk // LANES
    vmem = pl.BlockSpec(memory_space=pltpu.VMEM)
    hbm = pl.BlockSpec(memory_space=pltpu.HBM)
    return pl.pallas_call(
        functools.partial(kernel, n, tp, page),
        out_shape=pltpu.VMEM((rows, width), BF16),
        in_specs=[hbm] * 8,
        out_specs=vmem,
        scratch_shapes=[
            pltpu.VMEM((rows, width), BF16),
            pltpu.VMEM((1, width), F32),
            pltpu.VMEM((1, rows), jnp.int32),
            pltpu.VMEM(page_table.shape, jnp.int32),
            pltpu.VMEM((1, rows), jnp.int32),
            pltpu.VMEM((width, w_qkv.shape[2]), BF16),
            pltpu.VMEM((w_out.shape[1], width), BF16),
            pltpu.VMEM((tokens, entry), BF16),
            pltpu.VMEM((n, 2 * blocks * tp, LANES), BF16),
            pltpu.VMEM((n * (tp - 1), 2 * blocks * tp, LANES), BF16),
            pltpu.VMEM((n, 16, LANES), BF16),
            pltpu.VMEM((n, 16, LANES), BF16),
            pltpu.SemaphoreType.DMA((11,)),
            pltpu.SemaphoreType.DMA((2,)),
            pltpu.SemaphoreType.DMA((2,)),
        ],
        compiler_params=pltpu.CompilerParams(
            collective_id=0, has_side_effects=True, vmem_limit_bytes=60 * 1024 * 1024
        ),
    )(
        state,
        norm_gain.reshape(1, width),
        w_qkv.reshape(width, w_qkv.shape[2]),
        w_out[0],
        kv_cache.reshape(tokens, entry),
        lengths.reshape(1, rows),
        page_table,
        dest_slot.reshape(1, rows),
    )


def solution(mesh):
    placed = (
        P("req", None),
        P(),
        P(None, "tp", None),
        P("tp", None, None),
        P("req", "tp", None, None),
        P("req"),
        P("req", None),
        P("req"),
    )
    return jax.shard_map(
        functools.partial(local, mesh.shape["req"], mesh.shape["tp"]),
        mesh=mesh,
        in_specs=placed,
        out_specs=P("req", None),
        check_vma=False,
    )
```

```python
import functools
import math

import jax
import jax.numpy as jnp
from jax import lax
from jax.experimental import pallas as pl
from jax.experimental.pallas import tpu as pltpu
from jax.sharding import PartitionSpec as P

MESH = pl.DeviceIdType.MESH
LANES = 128
F32 = jnp.float32
BF16 = jnp.bfloat16


def iota(shape, axis):
    return lax.broadcasted_iota(jnp.int32, shape, axis)


def to_column(row):
    size = row.shape[1]
    eye = iota((size, size), 0) == iota((size, size), 1)
    return jnp.sum(jnp.where(eye, jnp.broadcast_to(row, (size, size)), 0.0), axis=1, keepdims=True)


def kernel(
    n,
    tp,
    page,
    state_hbm,
    gain_hbm,
    wqkv_hbm,
    wout_hbm,
    pool_hbm,
    len_hbm,
    table_hbm,
    dest_hbm,
    out_ref,
    state_ref,
    gain_ref,
    len_ref,
    table_ref,
    dest_ref,
    wqkv,
    wout,
    key_ref,
    value_ref,
    heads_out,
    heads_in,
    outgoing,
    incoming,
    load_sem,
    move_send,
    move_recv,
):
    rows, width = state_ref.shape
    group = wout.shape[0] // LANES
    halves = outgoing.shape[0]
    chunk = width // halves
    blocks = chunk // LANES
    depth = 2 * blocks
    tokens = key_ref.shape[0]
    page_count = tokens // page
    token_blocks = tokens // LANES
    per_block = LANES // page
    me = lax.axis_index("req")
    my_part = lax.axis_index("tp")

    def wrapped(value, size):
        return jnp.where(value >= size, value - size, value)

    pairs = [
        (state_hbm, state_ref),
        (gain_hbm, gain_ref),
        (len_hbm, len_ref),
        (table_hbm, table_ref),
        (dest_hbm, dest_ref),
    ]
    steps = 4
    step_rows = width // steps
    for step in range(steps):
        span = pl.ds(step * step_rows, step_rows)
        pairs.append((wqkv_hbm.at[span], wqkv.at[span]))
    pairs.append((pool_hbm.at[:, pl.ds(0, LANES)], key_ref))
    pairs.append((pool_hbm.at[:, pl.ds(LANES, LANES)], value_ref))
    pairs.append((wout_hbm, wout))
    copies = [
        pltpu.make_async_copy(src, dst, load_sem.at[slot]) for slot, (src, dst) in enumerate(pairs)
    ]
    for copy in copies:
        copy.start()
    small, loads = copies[:5], copies[5 : 5 + steps]
    load_keys, load_values, load_wout = copies[5 + steps :]

    barrier = pltpu.get_barrier_semaphore()

    def each_request_device(act):
        if n <= 32:
            for peer in range(n):
                act(peer)
        else:
            pl.loop(0, n)(act)

    def each_other(act):
        def visit(step):
            act(wrapped(me + step, n))

        if n <= 32:
            for step in range(1, n):
                visit(step)
        else:
            pl.loop(1, n)(visit)

    def device(peer, shift):
        return {"req": peer, "tp": wrapped(my_part + shift, tp)}

    def greet(shift, peer):
        pl.semaphore_signal(barrier, inc=1, device_id=device(peer, shift), device_id_type=MESH)

    each_other(functools.partial(greet, 0))
    for shift in range(1, tp):
        each_request_device(functools.partial(greet, shift))

    for copy in small[:2]:
        copy.wait()
    wide = state_ref[...].astype(F32)
    factor = lax.rsqrt(jnp.mean(wide * wide, axis=-1, keepdims=True) + 1e-05)
    normed = (wide * factor * gain_ref[...]).astype(BF16)

    def project(step):
        span = slice(step * step_rows, (step + 1) * step_rows)
        return jnp.dot(normed[:, span], wqkv[span, :], preferred_element_type=F32)

    for copy in small[2:]:
        copy.wait()
    loads[0].wait()
    proj = project(0)

    length = to_column(len_ref[...].astype(F32))
    lane = iota((rows, LANES), 1)
    half = LANES // 2
    index = lax.rem(lane, half).astype(F32)
    freqs = jnp.exp(-math.log(1000000.0) * 2.0 * index / LANES)
    angles = length * freqs
    cosine = jnp.cos(angles)
    sine = jnp.sin(angles)
    sine = jnp.where(lane < half, -sine, sine)

    loads[1].wait()
    proj = proj + project(1)

    padded = pl.cdiv(page_count, LANES) * LANES
    page_id = iota((rows, padded), 1)
    table = table_ref[...]
    entries = table.shape[1]
    live_count = jnp.zeros((rows, padded), F32)
    for entry in range(per_block):
        left = jnp.clip(length - float(entry * page), 0.0, float(page))
        live_count = live_count + jnp.where(page_id == table[:, entry : entry + 1], left, 0.0)
    is_long = length > float(LANES)
    long_length = jnp.sum(jnp.where(is_long, length, 0.0), axis=0, keepdims=True)
    long_table = jnp.sum(jnp.where(is_long, table.astype(F32), 0.0), axis=0, keepdims=True)
    long_pages = to_column(long_table).astype(jnp.int32)
    entry_id = iota((entries, 1), 0)
    left = jnp.clip(long_length - (entry_id * page).astype(F32), 0.0, float(page))
    left = jnp.where(entry_id >= per_block, left, 0.0)
    hit = iota((entries, padded), 1) == long_pages
    long_count = jnp.sum(jnp.where(hit, left, 0.0), axis=0, keepdims=True)
    live_count = live_count + jnp.where(is_long, long_count, 0.0)

    loads[2].wait()
    proj = proj + project(2)

    shifted = []
    for block in range(token_blocks):
        first = block * per_block
        base = first // LANES * LANES
        piece = live_count[:, base : base + LANES]
        if first != base:
            piece = pltpu.roll(piece, LANES - (first - base), 1)
        shifted.append(piece)
    spread = (iota((LANES, LANES), 0) == iota((LANES, LANES), 1) // page).astype(BF16)
    live_tokens = jnp.dot(
        jnp.concatenate(shifted, axis=0).astype(BF16), spread, preferred_element_type=F32
    )
    offset = lax.rem(lane, page).astype(F32)
    bias = [
        jnp.where(live_tokens[block * rows : (block + 1) * rows] > offset, 0.0, -jnp.inf)
        for block in range(token_blocks)
    ]
    bias = [jnp.concatenate([piece] * group, axis=0) for piece in bias]

    loads[3].wait()
    proj = proj + project(3)

    def rotated(values):
        return (values * cosine + pltpu.roll(values, half, 1) * sine).astype(BF16)

    heads = [rotated(proj[:, g * LANES : (g + 1) * LANES]) for g in range(group)]
    new_key = rotated(proj[:, group * LANES : (group + 1) * LANES])
    new_value = proj[:, (group + 1) * LANES :].astype(BF16)
    query = jnp.concatenate(heads, axis=0)

    load_keys.wait()
    scores = lax.dot_general(
        query, key_ref[...], (((1,), (1,)), ((), ())), preferred_element_type=F32
    )
    scores = jnp.concatenate(
        [
            scores[:, block * LANES : (block + 1) * LANES] + bias[block]
            for block in range(token_blocks)
        ],
        axis=1,
    )
    keys = jnp.concatenate([new_key] * group, axis=0).astype(F32)
    values = jnp.concatenate([new_value] * group, axis=0).astype(F32)
    score_new = jnp.sum(query.astype(F32) * keys, axis=1, keepdims=True)
    top = jnp.maximum(jnp.max(scores, axis=1, keepdims=True), score_new)
    scale = 1.0 / math.sqrt(LANES)
    weights = jnp.exp((scores - top) * scale)
    weight_new = jnp.exp((score_new - top) * scale)
    total = jnp.sum(weights, axis=1, keepdims=True) + weight_new
    weights = weights.astype(BF16)

    shift_bits = rows.bit_length() - 1
    target_row = lax.shift_right_logical(dest_ref[...], shift_bits).astype(F32)
    target = to_column(target_row)
    same = jnp.broadcast_to(target, (rows, rows)) == jnp.broadcast_to(target_row, (rows, rows))
    earlier = iota((rows, rows), 1) < iota((rows, rows), 0)
    rank = jnp.sum(jnp.where(same & earlier, 1.0, 0.0), axis=1, keepdims=True)
    source = (2 * me).astype(F32) - target
    source = jnp.where(source < 0, source + n, source)
    source = jnp.where(source >= n, source - n, source)

    def packing(parts, depth):
        flat = rows * parts
        first = (target * depth + rank * parts).astype(jnp.int32).astype(F32)
        picked = iota((rows, flat), 0) == lax.rem(iota((rows, flat), 1), rows)
        place = jnp.sum(jnp.where(picked, first, 0.0), axis=0, keepdims=True)
        place = place.astype(jnp.int32) + iota((1, flat), 1) // rows
        return (iota((n * depth, flat), 0) == place).astype(BF16)

    def unpacking(parts, depth):
        flat = rows * parts
        first = (source * depth + rank * parts).astype(jnp.int32)
        place = jnp.concatenate([first + part for part in range(parts)], axis=0)
        return (iota((flat, n * depth), 1) == place).astype(BF16)

    pack_heads = packing(1, 2)
    pack = packing(blocks, depth)

    load_values.wait()
    numer = jnp.dot(weights, value_ref[...], preferred_element_type=F32)
    numer = numer + weight_new.astype(BF16).astype(F32) * values
    attn = (numer / total).astype(BF16)

    attn = jnp.concatenate([attn[g * rows : (g + 1) * rows] for g in range(group)], axis=1)
    packed = jnp.dot(pack_heads, attn, preferred_element_type=F32)
    heads_out[...] = packed.reshape(heads_out.shape).astype(BF16)
    pl.semaphore_wait(barrier, n * tp - 1)

    def send_heads(peer):
        pltpu.make_async_remote_copy(
            src_ref=heads_out.at[peer],
            dst_ref=heads_in.at[me],
            send_sem=move_send.at[halves],
            recv_sem=move_recv.at[halves],
            device_id=device(peer, 0),
            device_id_type=MESH,
        ).start()

    each_other(send_heads)

    load_wout.wait()
    for part in range(halves):
        span = slice(part * chunk, (part + 1) * chunk)
        term = jnp.dot(attn, wout[:, span], preferred_element_type=F32)
        mixed = (state_ref[:, span].astype(F32) * (1.0 / (tp - 1)) + term).astype(BF16)
        stacked = jnp.concatenate(
            [mixed[:, b * LANES : (b + 1) * LANES] for b in range(blocks)], axis=0
        )
        packed = jnp.dot(pack, stacked, preferred_element_type=F32)
        outgoing[part] = packed.astype(BF16).reshape(n, depth, LANES)

        def send(shift, peer):
            pltpu.make_async_remote_copy(
                src_ref=outgoing.at[part, peer],
                dst_ref=incoming.at[part, (shift - 1) * n + me],
                send_sem=move_send.at[part],
                recv_sem=move_recv.at[part],
                device_id=device(peer, shift),
                device_id_type=MESH,
            ).start()

        for shift in range(1, tp):
            each_request_device(functools.partial(send, shift))

    unpack_heads = unpacking(1, 2)
    unpack = unpacking(blocks, depth)
    heads_in[me] = heads_out[me]
    others = heads_in.at[pl.ds(0, n - 1)]
    pltpu.make_async_copy(others, others, move_recv.at[halves]).wait()
    received = heads_in[...].astype(F32).reshape(2 * n, group * LANES).astype(BF16)
    arrived = jnp.dot(unpack_heads, received, preferred_element_type=F32).astype(BF16)
    own = jnp.dot(arrived, wout[...], preferred_element_type=F32)

    for part in range(halves):
        landed = incoming.at[part]
        pltpu.make_async_copy(landed, landed, move_recv.at[part]).wait()
        moved = None
        for origin in range(tp - 1):
            received = incoming[part, origin * n : (origin + 1) * n].reshape(n * depth, LANES)
            taken = jnp.dot(unpack, received, preferred_element_type=F32)
            moved = taken if moved is None else moved + taken
        for b in range(blocks):
            first = part * chunk + b * LANES
            out_ref[:, first : first + LANES] = (
                moved[b * rows : (b + 1) * rows] + own[:, first : first + LANES]
            ).astype(BF16)
    pltpu.make_async_copy(others, others, move_send.at[halves]).wait()
    for part in range(halves):
        sent = incoming.at[part]
        pltpu.make_async_copy(sent, sent, move_send.at[part]).wait()


def local(n, tp, state, norm_gain, w_qkv, w_out, kv_cache, lengths, page_table, dest_slot):
    rows, width = state.shape
    page_count, _, page, entry = kv_cache.shape
    tokens = page_count * page
    halves = 1
    blocks = width // halves // LANES
    vmem = pl.BlockSpec(memory_space=pltpu.VMEM)
    hbm = pl.BlockSpec(memory_space=pltpu.HBM)
    return pl.pallas_call(
        functools.partial(kernel, n, tp, page),
        out_shape=pltpu.VMEM((rows, width), BF16),
        in_specs=[hbm] * 8,
        out_specs=vmem,
        scratch_shapes=[
            pltpu.VMEM((rows, width), BF16),
            pltpu.VMEM((1, width), F32),
            pltpu.VMEM((1, rows), jnp.int32),
            pltpu.VMEM(page_table.shape, jnp.int32),
            pltpu.VMEM((1, rows), jnp.int32),
            pltpu.VMEM((width, w_qkv.shape[2]), BF16),
            pltpu.VMEM((w_out.shape[1], width), BF16),
            pltpu.VMEM((tokens, LANES), BF16),
            pltpu.VMEM((tokens, LANES), BF16),
            pltpu.VMEM((n, 2, w_out.shape[1]), BF16),
            pltpu.VMEM((n, 2, w_out.shape[1]), BF16),
            pltpu.VMEM((halves, n, 2 * blocks, LANES), BF16),
            pltpu.VMEM((halves, n * (tp - 1), 2 * blocks, LANES), BF16),
            pltpu.SemaphoreType.DMA((12,)),
            pltpu.SemaphoreType.DMA((halves + 1,)),
            pltpu.SemaphoreType.DMA((halves + 1,)),
        ],
        compiler_params=pltpu.CompilerParams(
            collective_id=0, has_side_effects=True, vmem_limit_bytes=60 * 1024 * 1024
        ),
    )(
        state,
        norm_gain.reshape(1, width),
        w_qkv.reshape(width, w_qkv.shape[2]),
        w_out[0],
        kv_cache.reshape(tokens, entry),
        lengths.reshape(1, rows),
        page_table,
        dest_slot.reshape(1, rows),
    )


def solution(mesh):
    placed = (
        P("req", None),
        P(),
        P(None, "tp", None),
        P("tp", None, None),
        P("req", "tp", None, None),
        P("req"),
        P("req", None),
        P("req"),
    )
    return jax.shard_map(
        functools.partial(local, mesh.shape["req"], mesh.shape["tp"]),
        mesh=mesh,
        in_specs=placed,
        out_specs=P("req", None),
        check_vma=False,
    )
```

```python
import functools
import math

import jax
import jax.numpy as jnp
from jax import lax
from jax.experimental import pallas as pl
from jax.experimental.pallas import tpu as pltpu
from jax.sharding import PartitionSpec as P

MESH = pl.DeviceIdType.MESH
LANES = 128
F32 = jnp.float32
BF16 = jnp.bfloat16


def iota(shape, axis):
    return lax.broadcasted_iota(jnp.int32, shape, axis)


def to_column(row):
    size = row.shape[1]
    eye = iota((size, size), 0) == iota((size, size), 1)
    return jnp.sum(jnp.where(eye, jnp.broadcast_to(row, (size, size)), 0.0), axis=1, keepdims=True)


def kernel(
    n,
    tp,
    page,
    state_hbm,
    gain_hbm,
    wqkv_hbm,
    wout_hbm,
    pool_hbm,
    len_hbm,
    table_hbm,
    dest_hbm,
    out_ref,
    state_ref,
    gain_ref,
    len_ref,
    table_ref,
    dest_ref,
    wqkv,
    wout,
    key_ref,
    value_ref,
    heads_out,
    heads_in,
    outgoing,
    incoming,
    load_sem,
    move_send,
    move_recv,
):
    rows, width = state_ref.shape
    group = wout.shape[0] // LANES
    wide_lanes = outgoing.shape[2]
    blocks = width // wide_lanes
    depth = 2 * blocks
    tokens = key_ref.shape[0]
    page_count = tokens // page
    token_blocks = tokens // LANES
    per_block = LANES // page
    me = lax.axis_index("req")
    my_part = lax.axis_index("tp")

    def wrapped(value, size):
        return jnp.where(value >= size, value - size, value)

    pairs = [
        (state_hbm, state_ref),
        (gain_hbm, gain_ref),
        (len_hbm, len_ref),
        (table_hbm, table_ref),
        (dest_hbm, dest_ref),
    ]
    steps = 4
    step_rows = width // steps
    for step in range(steps):
        span = pl.ds(step * step_rows, step_rows)
        pairs.append((wqkv_hbm.at[span], wqkv.at[span]))
    pairs.append((pool_hbm.at[:, pl.ds(0, LANES)], key_ref))
    pairs.append((pool_hbm.at[:, pl.ds(LANES, LANES)], value_ref))
    pairs.append((wout_hbm, wout))
    copies = [
        pltpu.make_async_copy(src, dst, load_sem.at[slot]) for slot, (src, dst) in enumerate(pairs)
    ]
    for copy in copies:
        copy.start()
    small, loads = copies[:5], copies[5 : 5 + steps]
    load_keys, load_values, load_wout = copies[5 + steps :]

    barrier = pltpu.get_barrier_semaphore()

    def each_request_device(act):
        if n <= 32:
            for peer in range(n):
                act(peer)
        else:
            pl.loop(0, n)(act)

    def each_other(act):
        def visit(step):
            act(wrapped(me + step, n))

        if n <= 32:
            for step in range(1, n):
                visit(step)
        else:
            pl.loop(1, n)(visit)

    def device(peer, shift):
        return {"req": peer, "tp": wrapped(my_part + shift, tp)}

    def greet(shift, peer):
        pl.semaphore_signal(barrier, inc=1, device_id=device(peer, shift), device_id_type=MESH)

    each_other(functools.partial(greet, 0))
    for shift in range(1, tp):
        each_request_device(functools.partial(greet, shift))

    for copy in small[:2]:
        copy.wait()
    wide = state_ref[...].astype(F32)
    factor = lax.rsqrt(jnp.mean(wide * wide, axis=-1, keepdims=True) + 1e-05)
    normed = (wide * factor * gain_ref[...]).astype(BF16)

    def project(step):
        span = slice(step * step_rows, (step + 1) * step_rows)
        return jnp.dot(normed[:, span], wqkv[span, :], preferred_element_type=F32)

    for copy in small[2:]:
        copy.wait()
    loads[0].wait()
    proj = project(0)

    length = to_column(len_ref[...].astype(F32))
    lane = iota((rows, LANES), 1)
    half = LANES // 2
    index = lax.rem(lane, half).astype(F32)
    freqs = jnp.exp(-math.log(1000000.0) * 2.0 * index / LANES)
    angles = length * freqs
    cosine = jnp.cos(angles)
    sine = jnp.sin(angles)
    sine = jnp.where(lane < half, -sine, sine)

    loads[1].wait()
    proj = proj + project(1)

    padded = pl.cdiv(page_count, LANES) * LANES
    page_id = iota((rows, padded), 1)
    table = table_ref[...]
    entries = table.shape[1]
    live_count = jnp.zeros((rows, padded), F32)
    for entry in range(per_block):
        left = jnp.clip(length - float(entry * page), 0.0, float(page))
        live_count = live_count + jnp.where(page_id == table[:, entry : entry + 1], left, 0.0)
    is_long = length > float(LANES)
    long_length = jnp.sum(jnp.where(is_long, length, 0.0), axis=0, keepdims=True)
    long_table = jnp.sum(jnp.where(is_long, table.astype(F32), 0.0), axis=0, keepdims=True)
    long_pages = to_column(long_table).astype(jnp.int32)
    entry_id = iota((entries, 1), 0)
    left = jnp.clip(long_length - (entry_id * page).astype(F32), 0.0, float(page))
    left = jnp.where(entry_id >= per_block, left, 0.0)
    hit = iota((entries, padded), 1) == long_pages
    long_count = jnp.sum(jnp.where(hit, left, 0.0), axis=0, keepdims=True)
    live_count = live_count + jnp.where(is_long, long_count, 0.0)

    loads[2].wait()
    proj = proj + project(2)

    shifted = []
    for block in range(token_blocks):
        first = block * per_block
        base = first // LANES * LANES
        piece = live_count[:, base : base + LANES]
        if first != base:
            piece = pltpu.roll(piece, LANES - (first - base), 1)
        shifted.append(piece)
    spread = (iota((LANES, LANES), 0) == iota((LANES, LANES), 1) // page).astype(BF16)
    live_tokens = jnp.dot(
        jnp.concatenate(shifted, axis=0).astype(BF16), spread, preferred_element_type=F32
    )
    offset = lax.rem(lane, page).astype(F32)
    bias = [
        jnp.where(live_tokens[block * rows : (block + 1) * rows] > offset, 0.0, -jnp.inf)
        for block in range(token_blocks)
    ]
    bias = [jnp.concatenate([piece] * group, axis=0) for piece in bias]

    loads[3].wait()
    proj = proj + project(3)

    def rotated(values):
        return (values * cosine + pltpu.roll(values, half, 1) * sine).astype(BF16)

    heads = [rotated(proj[:, g * LANES : (g + 1) * LANES]) for g in range(group)]
    new_key = rotated(proj[:, group * LANES : (group + 1) * LANES])
    new_value = proj[:, (group + 1) * LANES :].astype(BF16)
    query = jnp.concatenate(heads, axis=0)

    load_keys.wait()
    scores = lax.dot_general(
        query, key_ref[...], (((1,), (1,)), ((), ())), preferred_element_type=F32
    )
    scores = jnp.concatenate(
        [
            scores[:, block * LANES : (block + 1) * LANES] + bias[block]
            for block in range(token_blocks)
        ],
        axis=1,
    )
    keys = jnp.concatenate([new_key] * group, axis=0).astype(F32)
    values = jnp.concatenate([new_value] * group, axis=0).astype(F32)
    score_new = jnp.sum(query.astype(F32) * keys, axis=1, keepdims=True)
    top = jnp.maximum(jnp.max(scores, axis=1, keepdims=True), score_new)
    scale = 1.0 / math.sqrt(LANES)
    weights = jnp.exp((scores - top) * scale)
    weight_new = jnp.exp((score_new - top) * scale)
    total = jnp.sum(weights, axis=1, keepdims=True) + weight_new
    weights = weights.astype(BF16)

    shift_bits = rows.bit_length() - 1
    target_row = lax.shift_right_logical(dest_ref[...], shift_bits).astype(F32)
    target = to_column(target_row)
    same = jnp.broadcast_to(target, (rows, rows)) == jnp.broadcast_to(target_row, (rows, rows))
    earlier = iota((rows, rows), 1) < iota((rows, rows), 0)
    rank = jnp.sum(jnp.where(same & earlier, 1.0, 0.0), axis=1, keepdims=True)
    source = (2 * me).astype(F32) - target
    source = jnp.where(source < 0, source + n, source)
    source = jnp.where(source >= n, source - n, source)

    def packing(parts, depth):
        flat = rows * parts
        first = (target * depth + rank * parts).astype(jnp.int32).astype(F32)
        picked = iota((rows, flat), 0) == lax.rem(iota((rows, flat), 1), rows)
        place = jnp.sum(jnp.where(picked, first, 0.0), axis=0, keepdims=True)
        place = place.astype(jnp.int32) + iota((1, flat), 1) // rows
        return (iota((n * depth, flat), 0) == place).astype(BF16)

    def unpacking(parts, depth):
        flat = rows * parts
        first = (source * depth + rank * parts).astype(jnp.int32)
        place = jnp.concatenate([first + part for part in range(parts)], axis=0)
        return (iota((flat, n * depth), 1) == place).astype(BF16)

    pack_heads = packing(1, 2)
    pack = packing(blocks, depth)

    load_values.wait()
    numer = jnp.dot(weights, value_ref[...], preferred_element_type=F32)
    numer = numer + weight_new.astype(BF16).astype(F32) * values
    attn = (numer / total).astype(BF16)

    attn = jnp.concatenate([attn[g * rows : (g + 1) * rows] for g in range(group)], axis=1)
    packed = jnp.dot(pack_heads, attn, preferred_element_type=F32)
    heads_out[...] = packed.reshape(heads_out.shape).astype(BF16)
    pl.semaphore_wait(barrier, n * tp - 1)

    def send_heads(peer):
        pltpu.make_async_remote_copy(
            src_ref=heads_out.at[peer],
            dst_ref=heads_in.at[me],
            send_sem=move_send.at[0],
            recv_sem=move_recv.at[0],
            device_id=device(peer, 0),
            device_id_type=MESH,
        ).start()

    each_other(send_heads)

    load_wout.wait()
    term = jnp.dot(attn, wout[...], preferred_element_type=F32)
    mixed = (state_ref[...].astype(F32) * (1.0 / (tp - 1)) + term).astype(BF16)
    stacked = jnp.concatenate(
        [mixed[:, b * wide_lanes : (b + 1) * wide_lanes] for b in range(blocks)], axis=0
    )
    packed = jnp.dot(pack, stacked, preferred_element_type=F32)
    outgoing[...] = packed.astype(BF16).reshape(outgoing.shape)

    def send(shift, peer):
        pltpu.make_async_remote_copy(
            src_ref=outgoing.at[peer],
            dst_ref=incoming.at[(shift - 1) * n + me],
            send_sem=move_send.at[1],
            recv_sem=move_recv.at[1],
            device_id=device(peer, shift),
            device_id_type=MESH,
        ).start()

    for shift in range(1, tp):
        each_request_device(functools.partial(send, shift))

    unpack_heads = unpacking(1, 2)
    unpack = unpacking(blocks, depth)
    heads_in[me] = heads_out[me]
    others = heads_in.at[pl.ds(0, n - 1)]
    pltpu.make_async_copy(others, others, move_recv.at[0]).wait()
    received = heads_in[...].astype(F32).reshape(2 * n, group * LANES).astype(BF16)
    arrived = jnp.dot(unpack_heads, received, preferred_element_type=F32).astype(BF16)
    own = jnp.dot(arrived, wout[...], preferred_element_type=F32)

    pltpu.make_async_copy(incoming, incoming, move_recv.at[1]).wait()
    moved = None
    for origin in range(tp - 1):
        received = incoming[origin * n : (origin + 1) * n].reshape(n * depth, wide_lanes)
        taken = jnp.dot(unpack, received, preferred_element_type=F32)
        moved = taken if moved is None else moved + taken
    for b in range(blocks):
        span = slice(b * wide_lanes, (b + 1) * wide_lanes)
        out_ref[:, span] = (moved[b * rows : (b + 1) * rows] + own[:, span]).astype(BF16)
    pltpu.make_async_copy(others, others, move_send.at[0]).wait()
    pltpu.make_async_copy(incoming, incoming, move_send.at[1]).wait()


def local(n, tp, state, norm_gain, w_qkv, w_out, kv_cache, lengths, page_table, dest_slot):
    rows, width = state.shape
    page_count, _, page, entry = kv_cache.shape
    tokens = page_count * page
    wide_lanes = 2 * LANES
    depth = 2 * width // wide_lanes
    vmem = pl.BlockSpec(memory_space=pltpu.VMEM)
    hbm = pl.BlockSpec(memory_space=pltpu.HBM)
    return pl.pallas_call(
        functools.partial(kernel, n, tp, page),
        out_shape=pltpu.VMEM((rows, width), BF16),
        in_specs=[hbm] * 8,
        out_specs=vmem,
        scratch_shapes=[
            pltpu.VMEM((rows, width), BF16),
            pltpu.VMEM((1, width), F32),
            pltpu.VMEM((1, rows), jnp.int32),
            pltpu.VMEM(page_table.shape, jnp.int32),
            pltpu.VMEM((1, rows), jnp.int32),
            pltpu.VMEM((width, w_qkv.shape[2]), BF16),
            pltpu.VMEM((w_out.shape[1], width), BF16),
            pltpu.VMEM((tokens, LANES), BF16),
            pltpu.VMEM((tokens, LANES), BF16),
            pltpu.VMEM((n, 2, w_out.shape[1]), BF16),
            pltpu.VMEM((n, 2, w_out.shape[1]), BF16),
            pltpu.VMEM((n, depth, wide_lanes), BF16),
            pltpu.VMEM((n * (tp - 1), depth, wide_lanes), BF16),
            pltpu.SemaphoreType.DMA((12,)),
            pltpu.SemaphoreType.DMA((2,)),
            pltpu.SemaphoreType.DMA((2,)),
        ],
        compiler_params=pltpu.CompilerParams(
            collective_id=0, has_side_effects=True, vmem_limit_bytes=60 * 1024 * 1024
        ),
    )(
        state,
        norm_gain.reshape(1, width),
        w_qkv.reshape(width, w_qkv.shape[2]),
        w_out[0],
        kv_cache.reshape(tokens, entry),
        lengths.reshape(1, rows),
        page_table,
        dest_slot.reshape(1, rows),
    )


def solution(mesh):
    placed = (
        P("req", None),
        P(),
        P(None, "tp", None),
        P("tp", None, None),
        P("req", "tp", None, None),
        P("req"),
        P("req", None),
        P("req"),
    )
    return jax.shard_map(
        functools.partial(local, mesh.shape["req"], mesh.shape["tp"]),
        mesh=mesh,
        in_specs=placed,
        out_specs=P("req", None),
        check_vma=False,
    )
```

```python
import functools
import math

import jax
import jax.numpy as jnp
from jax import lax
from jax.experimental import pallas as pl
from jax.experimental.pallas import tpu as pltpu
from jax.sharding import PartitionSpec as P

MESH = pl.DeviceIdType.MESH
LANES = 128
F32 = jnp.float32
BF16 = jnp.bfloat16


def iota(shape, axis):
    return lax.broadcasted_iota(jnp.int32, shape, axis)


def to_column(row):
    size = row.shape[1]
    eye = iota((size, size), 0) == iota((size, size), 1)
    return jnp.sum(jnp.where(eye, jnp.broadcast_to(row, (size, size)), 0.0), axis=1, keepdims=True)


def kernel(
    n,
    tp,
    page,
    state_hbm,
    gain_hbm,
    wqkv_hbm,
    wout_hbm,
    pool_hbm,
    len_hbm,
    table_hbm,
    dest_hbm,
    out_ref,
    state_ref,
    gain_ref,
    len_ref,
    table_ref,
    dest_ref,
    wqkv,
    wout,
    key_ref,
    value_ref,
    heads_out,
    heads_in,
    outgoing,
    incoming,
    load_sem,
    move_send,
    move_recv,
):
    rows, width = state_ref.shape
    group = wout.shape[0] // LANES
    wide_lanes = outgoing.shape[2]
    blocks = width // wide_lanes
    depth = 2 * blocks
    tokens = key_ref.shape[0]
    page_count = tokens // page
    token_blocks = tokens // LANES
    per_block = LANES // page
    me = lax.axis_index("req")
    my_part = lax.axis_index("tp")

    def wrapped(value, size):
        return jnp.where(value >= size, value - size, value)

    pairs = [
        (state_hbm, state_ref),
        (gain_hbm, gain_ref),
        (len_hbm, len_ref),
        (table_hbm, table_ref),
        (dest_hbm, dest_ref),
    ]
    steps = 4
    step_rows = width // steps
    for step in range(steps):
        span = pl.ds(step * step_rows, step_rows)
        pairs.append((wqkv_hbm.at[span], wqkv.at[span]))
    pairs.append((pool_hbm.at[:, pl.ds(0, LANES)], key_ref))
    pairs.append((pool_hbm.at[:, pl.ds(LANES, LANES)], value_ref))
    pairs.append((wout_hbm, wout))
    copies = [
        pltpu.make_async_copy(src, dst, load_sem.at[slot]) for slot, (src, dst) in enumerate(pairs)
    ]
    for copy in copies:
        copy.start()
    small, loads = copies[:5], copies[5 : 5 + steps]
    load_keys, load_values, load_wout = copies[5 + steps :]

    barrier = pltpu.get_barrier_semaphore()

    def each_request_device(act):
        if n <= 32:
            for peer in range(n):
                act(peer)
        else:
            pl.loop(0, n)(act)

    def each_other(act):
        def visit(step):
            act(wrapped(me + step, n))

        if n <= 32:
            for step in range(1, n):
                visit(step)
        else:
            pl.loop(1, n)(visit)

    def device(peer, shift):
        return {"req": peer, "tp": wrapped(my_part + shift, tp)}

    def greet(shift, peer):
        pl.semaphore_signal(barrier, inc=1, device_id=device(peer, shift), device_id_type=MESH)

    each_other(functools.partial(greet, 0))
    for shift in range(1, tp):
        each_request_device(functools.partial(greet, shift))

    for copy in small[:2]:
        copy.wait()
    wide = state_ref[...].astype(F32)
    factor = lax.rsqrt(jnp.mean(wide * wide, axis=-1, keepdims=True) + 1e-05)
    normed = (wide * factor * gain_ref[...]).astype(BF16)

    def project(step):
        span = slice(step * step_rows, (step + 1) * step_rows)
        return jnp.dot(normed[:, span], wqkv[span, :], preferred_element_type=F32)

    for copy in small[2:]:
        copy.wait()
    loads[0].wait()
    proj = project(0)

    length = to_column(len_ref[...].astype(F32))
    lane = iota((rows, LANES), 1)
    half = LANES // 2
    index = lax.rem(lane, half).astype(F32)
    freqs = jnp.exp(-math.log(1000000.0) * 2.0 * index / LANES)
    angles = length * freqs
    cosine = jnp.cos(angles)
    sine = jnp.sin(angles)
    sine = jnp.where(lane < half, -sine, sine)

    loads[1].wait()
    proj = proj + project(1)

    padded = pl.cdiv(page_count, LANES) * LANES
    page_id = iota((rows, padded), 1)
    table = table_ref[...]
    entries = table.shape[1]
    live_count = jnp.zeros((rows, padded), F32)
    for entry in range(per_block):
        left = jnp.clip(length - float(entry * page), 0.0, float(page))
        live_count = live_count + jnp.where(page_id == table[:, entry : entry + 1], left, 0.0)
    is_long = length > float(LANES)
    long_length = jnp.sum(jnp.where(is_long, length, 0.0), axis=0, keepdims=True)
    long_table = jnp.sum(jnp.where(is_long, table.astype(F32), 0.0), axis=0, keepdims=True)
    long_pages = to_column(long_table).astype(jnp.int32)
    entry_id = iota((entries, 1), 0)
    left = jnp.clip(long_length - (entry_id * page).astype(F32), 0.0, float(page))
    left = jnp.where(entry_id >= per_block, left, 0.0)
    hit = iota((entries, padded), 1) == long_pages
    long_count = jnp.sum(jnp.where(hit, left, 0.0), axis=0, keepdims=True)
    live_count = live_count + jnp.where(is_long, long_count, 0.0)

    loads[2].wait()
    proj = proj + project(2)

    shifted = []
    for block in range(token_blocks):
        first = block * per_block
        base = first // LANES * LANES
        piece = live_count[:, base : base + LANES]
        if first != base:
            piece = pltpu.roll(piece, LANES - (first - base), 1)
        shifted.append(piece)
    spread = (iota((LANES, LANES), 0) == iota((LANES, LANES), 1) // page).astype(BF16)
    live_tokens = jnp.dot(
        jnp.concatenate(shifted, axis=0).astype(BF16), spread, preferred_element_type=F32
    )
    offset = lax.rem(lane, page).astype(F32)
    bias = [
        jnp.where(live_tokens[block * rows : (block + 1) * rows] > offset, 0.0, -jnp.inf)
        for block in range(token_blocks)
    ]
    bias = [jnp.concatenate([piece] * group, axis=0) for piece in bias]

    loads[3].wait()
    proj = proj + project(3)

    def rotated(values):
        return (values * cosine + pltpu.roll(values, half, 1) * sine).astype(BF16)

    heads = [rotated(proj[:, g * LANES : (g + 1) * LANES]) for g in range(group)]
    new_key = rotated(proj[:, group * LANES : (group + 1) * LANES])
    new_value = proj[:, (group + 1) * LANES :].astype(BF16)
    query = jnp.concatenate(heads, axis=0)

    load_keys.wait()
    scores = lax.dot_general(
        query, key_ref[...], (((1,), (1,)), ((), ())), preferred_element_type=F32
    )
    scores = jnp.concatenate(
        [
            scores[:, block * LANES : (block + 1) * LANES] + bias[block]
            for block in range(token_blocks)
        ],
        axis=1,
    )
    keys = jnp.concatenate([new_key] * group, axis=0).astype(F32)
    values = jnp.concatenate([new_value] * group, axis=0).astype(F32)
    score_new = jnp.sum(query.astype(F32) * keys, axis=1, keepdims=True)
    top = jnp.maximum(jnp.max(scores, axis=1, keepdims=True), score_new)
    scale = 1.0 / math.sqrt(LANES)
    weights = jnp.exp((scores - top) * scale)
    weight_new = jnp.exp((score_new - top) * scale)
    total = jnp.sum(weights, axis=1, keepdims=True) + weight_new
    weights = weights.astype(BF16)

    shift_bits = rows.bit_length() - 1
    target_row = lax.shift_right_logical(dest_ref[...], shift_bits).astype(F32)
    target = to_column(target_row)
    same = jnp.broadcast_to(target, (rows, rows)) == jnp.broadcast_to(target_row, (rows, rows))
    earlier = iota((rows, rows), 1) < iota((rows, rows), 0)
    rank = jnp.sum(jnp.where(same & earlier, 1.0, 0.0), axis=1, keepdims=True)
    source = (2 * me).astype(F32) - target
    source = jnp.where(source < 0, source + n, source)
    source = jnp.where(source >= n, source - n, source)

    def packing(parts, depth):
        flat = rows * parts
        first = (target * depth + rank * parts).astype(jnp.int32).astype(F32)
        picked = iota((rows, flat), 0) == lax.rem(iota((rows, flat), 1), rows)
        place = jnp.sum(jnp.where(picked, first, 0.0), axis=0, keepdims=True)
        place = place.astype(jnp.int32) + iota((1, flat), 1) // rows
        return (iota((n * depth, flat), 0) == place).astype(BF16)

    def unpacking(parts, depth):
        flat = rows * parts
        first = (source * depth + rank * parts).astype(jnp.int32)
        place = jnp.concatenate([first + part for part in range(parts)], axis=0)
        return (iota((flat, n * depth), 1) == place).astype(BF16)

    pack_heads = packing(1, 2)
    pack = packing(blocks, depth)

    load_values.wait()
    load_wout.wait()
    numer = jnp.dot(weights, value_ref[...], preferred_element_type=F32)
    numer = numer + weight_new.astype(BF16).astype(F32) * values
    attn = (numer / total).astype(BF16)

    attn = jnp.concatenate([attn[g * rows : (g + 1) * rows] for g in range(group)], axis=1)
    packed = jnp.dot(pack_heads, attn, preferred_element_type=F32)
    heads_out[...] = packed.reshape(heads_out.shape).astype(BF16)

    def send_heads(peer):
        pltpu.make_async_remote_copy(
            src_ref=heads_out.at[peer],
            dst_ref=heads_in.at[me],
            send_sem=move_send.at[0],
            recv_sem=move_recv.at[0],
            device_id=device(peer, 0),
            device_id_type=MESH,
        ).start()


    term = jnp.dot(attn, wout[...], preferred_element_type=F32)
    mixed = (state_ref[...].astype(F32) * (1.0 / (tp - 1)) + term).astype(BF16)
    stacked = jnp.concatenate(
        [mixed[:, b * wide_lanes : (b + 1) * wide_lanes] for b in range(blocks)], axis=0
    )
    def send(shift, peer):
        pltpu.make_async_remote_copy(
            src_ref=outgoing.at[peer],
            dst_ref=incoming.at[(shift - 1) * n + me],
            send_sem=move_send.at[1],
            recv_sem=move_recv.at[1],
            device_id=device(peer, shift),
            device_id_type=MESH,
        ).start()

    ahead = 2
    packed = jnp.dot(pack[: ahead * depth], stacked, preferred_element_type=F32)
    outgoing[:ahead] = packed.astype(BF16).reshape(ahead, depth, wide_lanes)
    pl.semaphore_wait(barrier, n * tp - 1)
    for shift in range(1, tp):
        for peer in range(ahead):
            send(shift, peer)
    packed = jnp.dot(pack[ahead * depth :], stacked, preferred_element_type=F32)
    outgoing[ahead:] = packed.astype(BF16).reshape(n - ahead, depth, wide_lanes)
    each_other(send_heads)
    for shift in range(1, tp):
        if n <= 32:
            for peer in range(ahead, n):
                send(shift, peer)
        else:
            pl.loop(ahead, n)(functools.partial(send, shift))

    unpack_heads = unpacking(1, 2)
    unpack = unpacking(blocks, depth)
    heads_in[me] = heads_out[me]
    others = heads_in.at[pl.ds(0, n - 1)]
    pltpu.make_async_copy(others, others, move_recv.at[0]).wait()
    received = heads_in[...].astype(F32).reshape(2 * n, group * LANES).astype(BF16)
    arrived = jnp.dot(unpack_heads, received, preferred_element_type=F32).astype(BF16)
    own = jnp.dot(arrived, wout[...], preferred_element_type=F32)

    pltpu.make_async_copy(others, others, move_send.at[0]).wait()
    pltpu.make_async_copy(incoming, incoming, move_send.at[1]).wait()
    pltpu.make_async_copy(incoming, incoming, move_recv.at[1]).wait()
    moved = None
    for origin in range(tp - 1):
        received = incoming[origin * n : (origin + 1) * n].reshape(n * depth, wide_lanes)
        taken = jnp.dot(unpack, received, preferred_element_type=F32)
        moved = taken if moved is None else moved + taken
    for b in range(blocks):
        span = slice(b * wide_lanes, (b + 1) * wide_lanes)
        out_ref[:, span] = (moved[b * rows : (b + 1) * rows] + own[:, span]).astype(BF16)


def local(n, tp, state, norm_gain, w_qkv, w_out, kv_cache, lengths, page_table, dest_slot):
    rows, width = state.shape
    page_count, _, page, entry = kv_cache.shape
    tokens = page_count * page
    wide_lanes = 2 * LANES
    depth = 2 * width // wide_lanes
    vmem = pl.BlockSpec(memory_space=pltpu.VMEM)
    hbm = pl.BlockSpec(memory_space=pltpu.HBM)
    return pl.pallas_call(
        functools.partial(kernel, n, tp, page),
        out_shape=pltpu.VMEM((rows, width), BF16),
        in_specs=[hbm] * 8,
        out_specs=vmem,
        scratch_shapes=[
            pltpu.VMEM((rows, width), BF16),
            pltpu.VMEM((1, width), F32),
            pltpu.VMEM((1, rows), jnp.int32),
            pltpu.VMEM(page_table.shape, jnp.int32),
            pltpu.VMEM((1, rows), jnp.int32),
            pltpu.VMEM((width, w_qkv.shape[2]), BF16),
            pltpu.VMEM((w_out.shape[1], width), BF16),
            pltpu.VMEM((tokens, LANES), BF16),
            pltpu.VMEM((tokens, LANES), BF16),
            pltpu.VMEM((n, 2, w_out.shape[1]), BF16),
            pltpu.VMEM((n, 2, w_out.shape[1]), BF16),
            pltpu.VMEM((n, depth, wide_lanes), BF16),
            pltpu.VMEM((n * (tp - 1), depth, wide_lanes), BF16),
            pltpu.SemaphoreType.DMA((12,)),
            pltpu.SemaphoreType.DMA((2,)),
            pltpu.SemaphoreType.DMA((2,)),
        ],
        compiler_params=pltpu.CompilerParams(
            collective_id=0, has_side_effects=True, vmem_limit_bytes=60 * 1024 * 1024
        ),
    )(
        state,
        norm_gain.reshape(1, width),
        w_qkv.reshape(width, w_qkv.shape[2]),
        w_out[0],
        kv_cache.reshape(tokens, entry),
        lengths.reshape(1, rows),
        page_table,
        dest_slot.reshape(1, rows),
    )


def solution(mesh):
    placed = (
        P("req", None),
        P(),
        P(None, "tp", None),
        P("tp", None, None),
        P("req", "tp", None, None),
        P("req"),
        P("req", None),
        P("req"),
    )
    return jax.shard_map(
        functools.partial(local, mesh.shape["req"], mesh.shape["tp"]),
        mesh=mesh,
        in_specs=placed,
        out_specs=P("req", None),
        check_vma=False,
    )
```

```python
import functools
import math

import jax
import jax.numpy as jnp
from jax import lax
from jax.experimental import pallas as pl
from jax.experimental.pallas import tpu as pltpu
from jax.sharding import PartitionSpec as P

MESH = pl.DeviceIdType.MESH
LANES = 128
F32 = jnp.float32
BF16 = jnp.bfloat16


def iota(shape, axis):
    return lax.broadcasted_iota(jnp.int32, shape, axis)


def to_column(row):
    size = row.shape[1]
    eye = iota((size, size), 0) == iota((size, size), 1)
    return jnp.sum(jnp.where(eye, jnp.broadcast_to(row, (size, size)), 0.0), axis=1, keepdims=True)


def kernel(
    n,
    tp,
    page,
    state_hbm,
    gain_hbm,
    wqkv_hbm,
    wout_hbm,
    pool_hbm,
    len_hbm,
    table_hbm,
    dest_hbm,
    out_ref,
    state_ref,
    gain_ref,
    len_ref,
    table_ref,
    dest_ref,
    wqkv,
    wout,
    key_ref,
    value_ref,
    heads_out,
    heads_in,
    outgoing,
    incoming,
    load_sem,
    move_send,
    move_recv,
):
    rows, width = state_ref.shape
    group = wout.shape[0] // LANES
    wide_lanes = outgoing.shape[2]
    blocks = width // wide_lanes
    depth = 2 * blocks
    tokens = pool_hbm.shape[0]
    front = key_ref.shape[0]
    back = tokens - front
    page_count = tokens // page
    token_blocks = tokens // LANES
    per_block = LANES // page
    me = lax.axis_index("req")
    my_part = lax.axis_index("tp")

    def wrapped(value, size):
        return jnp.where(value >= size, value - size, value)

    pairs = [
        (state_hbm, state_ref),
        (gain_hbm, gain_ref),
        (len_hbm, len_ref),
        (table_hbm, table_ref),
        (dest_hbm, dest_ref),
    ]
    steps = 4
    step_rows = width // steps
    for step in range(steps):
        span = pl.ds(step * step_rows, step_rows)
        pairs.append((wqkv_hbm.at[span], wqkv.at[span]))
    pairs.append((pool_hbm.at[pl.ds(0, front), pl.ds(0, LANES)], key_ref.at[:, pl.ds(0, LANES)]))
    pairs.append(
        (
            pool_hbm.at[pl.ds(front, back), pl.ds(0, LANES)],
            key_ref.at[pl.ds(0, back), pl.ds(LANES, LANES)],
        )
    )
    pairs.append((pool_hbm.at[:, pl.ds(LANES, LANES)], value_ref))
    pairs.append((wout_hbm, wout))
    copies = [
        pltpu.make_async_copy(src, dst, load_sem.at[slot]) for slot, (src, dst) in enumerate(pairs)
    ]
    for copy in copies:
        copy.start()
    small, loads = copies[:5], copies[5 : 5 + steps]
    load_keys, load_rest, load_values, load_wout = copies[5 + steps :]

    barrier = pltpu.get_barrier_semaphore()

    def each_request_device(act):
        if n <= 32:
            for peer in range(n):
                act(peer)
        else:
            pl.loop(0, n)(act)

    def each_other(act):
        def visit(step):
            act(wrapped(me + step, n))

        if n <= 32:
            for step in range(1, n):
                visit(step)
        else:
            pl.loop(1, n)(visit)

    def device(peer, shift):
        return {"req": peer, "tp": wrapped(my_part + shift, tp)}

    def greet(shift, peer):
        pl.semaphore_signal(barrier, inc=1, device_id=device(peer, shift), device_id_type=MESH)

    each_other(functools.partial(greet, 0))
    for shift in range(1, tp):
        each_request_device(functools.partial(greet, shift))

    if back < front:
        key_ref[back:, LANES:] = jnp.zeros((front - back, LANES), BF16)
    for copy in small[:2]:
        copy.wait()
    wide = state_ref[...].astype(F32)
    factor = lax.rsqrt(jnp.mean(wide * wide, axis=-1, keepdims=True) + 1e-05)
    normed = (wide * factor * gain_ref[...]).astype(BF16)

    def project(step):
        span = slice(step * step_rows, (step + 1) * step_rows)
        return jnp.dot(normed[:, span], wqkv[span, :], preferred_element_type=F32)

    for copy in small[2:]:
        copy.wait()
    loads[0].wait()
    proj = project(0)

    length = to_column(len_ref[...].astype(F32))
    lane = iota((rows, LANES), 1)
    half = LANES // 2
    index = lax.rem(lane, half).astype(F32)
    freqs = jnp.exp(-math.log(1000000.0) * 2.0 * index / LANES)
    angles = length * freqs
    cosine = jnp.cos(angles)
    sine = jnp.sin(angles)
    sine = jnp.where(lane < half, -sine, sine)

    loads[1].wait()
    proj = proj + project(1)

    padded = pl.cdiv(page_count, LANES) * LANES
    page_id = iota((rows, padded), 1)
    table = table_ref[...]
    entries = table.shape[1]
    live_count = jnp.zeros((rows, padded), F32)
    for entry in range(per_block):
        left = jnp.clip(length - float(entry * page), 0.0, float(page))
        live_count = live_count + jnp.where(page_id == table[:, entry : entry + 1], left, 0.0)
    is_long = length > float(LANES)
    long_length = jnp.sum(jnp.where(is_long, length, 0.0), axis=0, keepdims=True)
    long_table = jnp.sum(jnp.where(is_long, table.astype(F32), 0.0), axis=0, keepdims=True)
    long_pages = to_column(long_table).astype(jnp.int32)
    entry_id = iota((entries, 1), 0)
    left = jnp.clip(long_length - (entry_id * page).astype(F32), 0.0, float(page))
    left = jnp.where(entry_id >= per_block, left, 0.0)
    hit = iota((entries, padded), 1) == long_pages
    long_count = jnp.sum(jnp.where(hit, left, 0.0), axis=0, keepdims=True)
    live_count = live_count + jnp.where(is_long, long_count, 0.0)

    loads[2].wait()
    proj = proj + project(2)

    shifted = []
    for block in range(token_blocks):
        first = block * per_block
        base = first // LANES * LANES
        piece = live_count[:, base : base + LANES]
        if first != base:
            piece = pltpu.roll(piece, LANES - (first - base), 1)
        shifted.append(piece)
    spread = (iota((LANES, LANES), 0) == iota((LANES, LANES), 1) // page).astype(BF16)
    live_tokens = jnp.dot(
        jnp.concatenate(shifted, axis=0).astype(BF16), spread, preferred_element_type=F32
    )
    offset = lax.rem(lane, page).astype(F32)
    bias = [
        jnp.where(live_tokens[block * rows : (block + 1) * rows] > offset, 0.0, -jnp.inf)
        for block in range(token_blocks)
    ]
    bias = [jnp.concatenate([piece] * group, axis=0) for piece in bias]

    loads[3].wait()
    proj = proj + project(3)

    def rotated(values):
        return (values * cosine + pltpu.roll(values, half, 1) * sine).astype(BF16)

    heads = [rotated(proj[:, g * LANES : (g + 1) * LANES]) for g in range(group)]
    new_key = rotated(proj[:, group * LANES : (group + 1) * LANES])
    new_value = proj[:, (group + 1) * LANES :].astype(BF16)
    query = jnp.concatenate(heads, axis=0)

    load_keys.wait()
    load_rest.wait()
    blank = jnp.zeros_like(query)
    paired = jnp.concatenate(
        [jnp.concatenate([query, blank], axis=1), jnp.concatenate([blank, query], axis=1)], axis=0
    )
    both = lax.dot_general(
        paired, key_ref[...], (((1,), (1,)), ((), ())), preferred_element_type=F32
    )
    heads_rows = query.shape[0]
    scores = jnp.concatenate([both[:heads_rows], both[heads_rows:, :back]], axis=1)
    scores = jnp.concatenate(
        [
            scores[:, block * LANES : (block + 1) * LANES] + bias[block]
            for block in range(token_blocks)
        ],
        axis=1,
    )
    keys = jnp.concatenate([new_key] * group, axis=0).astype(F32)
    values = jnp.concatenate([new_value] * group, axis=0).astype(F32)
    score_new = jnp.sum(query.astype(F32) * keys, axis=1, keepdims=True)
    top = jnp.maximum(jnp.max(scores, axis=1, keepdims=True), score_new)
    scale = 1.0 / math.sqrt(LANES)
    weights = jnp.exp((scores - top) * scale)
    weight_new = jnp.exp((score_new - top) * scale)
    total = jnp.sum(weights, axis=1, keepdims=True) + weight_new
    weights = weights.astype(BF16)

    shift_bits = rows.bit_length() - 1
    target_row = lax.shift_right_logical(dest_ref[...], shift_bits).astype(F32)
    target = to_column(target_row)
    same = jnp.broadcast_to(target, (rows, rows)) == jnp.broadcast_to(target_row, (rows, rows))
    earlier = iota((rows, rows), 1) < iota((rows, rows), 0)
    rank = jnp.sum(jnp.where(same & earlier, 1.0, 0.0), axis=1, keepdims=True)
    source = (2 * me).astype(F32) - target
    source = jnp.where(source < 0, source + n, source)
    source = jnp.where(source >= n, source - n, source)

    def packing(parts, depth):
        flat = rows * parts
        first = (target * depth + rank * parts).astype(jnp.int32).astype(F32)
        picked = iota((rows, flat), 0) == lax.rem(iota((rows, flat), 1), rows)
        place = jnp.sum(jnp.where(picked, first, 0.0), axis=0, keepdims=True)
        place = place.astype(jnp.int32) + iota((1, flat), 1) // rows
        return (iota((n * depth, flat), 0) == place).astype(BF16)

    def unpacking(parts, depth):
        flat = rows * parts
        first = (source * depth + rank * parts).astype(jnp.int32)
        place = jnp.concatenate([first + part for part in range(parts)], axis=0)
        return (iota((flat, n * depth), 1) == place).astype(BF16)

    pack_heads = packing(1, 2)
    pack = packing(blocks, depth)

    load_values.wait()
    load_wout.wait()
    numer = jnp.dot(weights, value_ref[...], preferred_element_type=F32)
    numer = numer + weight_new.astype(BF16).astype(F32) * values
    attn = (numer / total).astype(BF16)

    attn = jnp.concatenate([attn[g * rows : (g + 1) * rows] for g in range(group)], axis=1)

    def send_heads(peer):
        pltpu.make_async_remote_copy(
            src_ref=heads_out.at[peer],
            dst_ref=heads_in.at[me],
            send_sem=move_send.at[0],
            recv_sem=move_recv.at[0],
            device_id=device(peer, 0),
            device_id_type=MESH,
        ).start()


    term = jnp.dot(attn, wout[...], preferred_element_type=F32)
    mixed = (state_ref[...].astype(F32) * (1.0 / (tp - 1)) + term).astype(BF16)
    stacked = jnp.concatenate(
        [mixed[:, b * wide_lanes : (b + 1) * wide_lanes] for b in range(blocks)], axis=0
    )
    def send(shift, peer):
        pltpu.make_async_remote_copy(
            src_ref=outgoing.at[peer],
            dst_ref=incoming.at[(shift - 1) * n + me],
            send_sem=move_send.at[1],
            recv_sem=move_recv.at[1],
            device_id=device(peer, shift),
            device_id_type=MESH,
        ).start()

    ahead = 2
    packed = jnp.dot(pack[: ahead * depth], stacked, preferred_element_type=F32)
    outgoing[:ahead] = packed.reshape(ahead, depth, wide_lanes).astype(BF16)
    pl.semaphore_wait(barrier, n * tp - 1)
    for shift in range(1, tp):
        for peer in range(ahead):
            send(shift, peer)
    packed = jnp.dot(pack_heads, attn, preferred_element_type=F32)
    heads_out[...] = packed.reshape(heads_out.shape).astype(BF16)
    packed = jnp.dot(pack[ahead * depth :], stacked, preferred_element_type=F32)
    outgoing[ahead:] = packed.reshape(n - ahead, depth, wide_lanes).astype(BF16)
    each_other(send_heads)
    for shift in range(1, tp):
        if n <= 32:
            for peer in range(ahead, n):
                send(shift, peer)
        else:
            pl.loop(ahead, n)(functools.partial(send, shift))

    unpack_heads = unpacking(1, 2)
    unpack = unpacking(blocks, depth)
    heads_in[me] = heads_out[me]
    others = heads_in.at[pl.ds(0, n - 1)]
    pltpu.make_async_copy(others, others, move_recv.at[0]).wait()
    received = heads_in[...].astype(F32).reshape(2 * n, group * LANES).astype(BF16)
    arrived = jnp.dot(unpack_heads, received, preferred_element_type=F32).astype(BF16)
    own = jnp.dot(arrived, wout[...], preferred_element_type=F32)

    pltpu.make_async_copy(others, others, move_send.at[0]).wait()
    pltpu.make_async_copy(incoming, incoming, move_send.at[1]).wait()
    pltpu.make_async_copy(incoming, incoming, move_recv.at[1]).wait()
    moved = None
    for origin in range(tp - 1):
        received = incoming[origin * n : (origin + 1) * n].astype(F32)
        received = received.reshape(n * depth, wide_lanes).astype(BF16)
        taken = jnp.dot(unpack, received, preferred_element_type=F32)
        moved = taken if moved is None else moved + taken
    for b in range(blocks):
        span = slice(b * wide_lanes, (b + 1) * wide_lanes)
        out_ref[:, span] = (moved[b * rows : (b + 1) * rows] + own[:, span]).astype(BF16)


def local(n, tp, state, norm_gain, w_qkv, w_out, kv_cache, lengths, page_table, dest_slot):
    rows, width = state.shape
    page_count, _, page, entry = kv_cache.shape
    tokens = page_count * page
    wide_lanes = 4 * LANES
    depth = 2 * width // wide_lanes
    vmem = pl.BlockSpec(memory_space=pltpu.VMEM)
    hbm = pl.BlockSpec(memory_space=pltpu.HBM)
    return pl.pallas_call(
        functools.partial(kernel, n, tp, page),
        out_shape=pltpu.VMEM((rows, width), BF16),
        in_specs=[hbm] * 8,
        out_specs=vmem,
        scratch_shapes=[
            pltpu.VMEM((rows, width), BF16),
            pltpu.VMEM((1, width), F32),
            pltpu.VMEM((1, rows), jnp.int32),
            pltpu.VMEM(page_table.shape, jnp.int32),
            pltpu.VMEM((1, rows), jnp.int32),
            pltpu.VMEM((width, w_qkv.shape[2]), BF16),
            pltpu.VMEM((w_out.shape[1], width), BF16),
            pltpu.VMEM((pl.cdiv(tokens // LANES, 2) * LANES, 2 * LANES), BF16),
            pltpu.VMEM((tokens, LANES), BF16),
            pltpu.VMEM((n, 2, w_out.shape[1]), BF16),
            pltpu.VMEM((n, 2, w_out.shape[1]), BF16),
            pltpu.VMEM((n, depth, wide_lanes), BF16),
            pltpu.VMEM((n * (tp - 1), depth, wide_lanes), BF16),
            pltpu.SemaphoreType.DMA((13,)),
            pltpu.SemaphoreType.DMA((2,)),
            pltpu.SemaphoreType.DMA((2,)),
        ],
        compiler_params=pltpu.CompilerParams(
            collective_id=0, has_side_effects=True, vmem_limit_bytes=60 * 1024 * 1024
        ),
    )(
        state,
        norm_gain.reshape(1, width),
        w_qkv.reshape(width, w_qkv.shape[2]),
        w_out[0],
        kv_cache.reshape(tokens, entry),
        lengths.reshape(1, rows),
        page_table,
        dest_slot.reshape(1, rows),
    )


def solution(mesh):
    placed = (
        P("req", None),
        P(),
        P(None, "tp", None),
        P("tp", None, None),
        P("req", "tp", None, None),
        P("req"),
        P("req", None),
        P("req"),
    )
    return jax.shard_map(
        functools.partial(local, mesh.shape["req"], mesh.shape["tp"]),
        mesh=mesh,
        in_specs=placed,
        out_specs=P("req", None),
        check_vma=False,
    )
```
